256 devices in a mesh: draw: 32 (over x, z), vocab: 8 (over y, core).
Axes of the slice: x: 4, y: 4, z: 8, core: 2. Of those that a mesh axis runs over, the one named last changes fastest.
Arguments:
- hidden: bfloat16 [64, 384, 896], P('draw'), may hold values from -256 to 256
- unembed: bfloat16 [896, 76032], P('draw', 'vocab'), may hold values from -1 to 1
- targets: int32 [384], replicated, may hold values from 0 to 76031
Outputs:
- influence: float32 [256, 128], P('draw')
The draws below stay inside these ranges and needn't reach their ends.
All inputs are finite; a program needn't handle non-finite values.
Results may differ from the reference program's by a relative error of at most 0.0003.
Values may be sent and summed in bfloat16 or wider, within the bound.
No kernel may reach another device: no remote copies, remote signals or barrier semaphores. Data moves between devices by JAX's collectives and lax.ppermute only.
A program may use at most 192 MiB of HBM per device.

```python
import jax
import jax.numpy as jnp
from jax import lax

D = 896
V = 76032
TRAIN = 256
QUERY = 128
DRAWS = 64
TOK = 384


def pick_slots(key):
    slot_key = jax.random.fold_in(key, 101)
    key_first = jax.random.fold_in(slot_key, 0)
    key_one = jax.random.fold_in(slot_key, 2)
    key_two = jax.random.fold_in(slot_key, 3)
    key_three = jax.random.fold_in(slot_key, 4)
    first_column = jax.random.randint(key_first, (), 0, V)
    token_one = jax.random.randint(key_one, (), 0, TRAIN // 2)
    token_two = jax.random.randint(key_two, (), TRAIN // 2, TRAIN)
    token_three = jax.random.randint(key_three, (), TRAIN, TRAIN + QUERY)
    return (first_column, jnp.stack([token_one, token_two, token_three]))


def base_weight(key):
    values_drawn = jax.random.normal(jax.random.fold_in(key, 202), (D, V), jnp.float32)
    return jnp.clip(values_drawn, -6.0, 6.0) * D ** (-0.5)


def draw_unembed(key, part):
    matrix = base_weight(key)
    return matrix.astype(jnp.bfloat16)


def draw_hidden(key, part):
    hidden_key = jax.random.fold_in(key, 303)
    values_drawn = jnp.clip(jax.random.normal(hidden_key, (DRAWS, TOK, D), jnp.float32), -6.0, 6.0) * 3.0
    return values_drawn.astype(jnp.bfloat16)


def draw_targets(key, part):
    first_column, slot_tokens = pick_slots(key)
    target_ids = jax.random.randint(jax.random.fold_in(key, 404), (TOK,), 0, V)
    marked = jnp.any(jnp.arange(TOK)[:, None] == slot_tokens[None, :], axis=1)
    return jnp.where(marked, first_column, target_ids).astype(jnp.int32)


def setup_inputs(seed: int = 0) -> dict:
    key_of = jax.random.split(jax.random.key(seed), 4)
    return {
        "hidden": draw_hidden(jax.random.fold_in(key_of[3], 71), 0),
        "unembed": draw_unembed(jax.random.fold_in(key_of[3], 71), 0),
        "targets": draw_targets(jax.random.fold_in(key_of[3], 71), 0),
    }


def token_losses(token_rows, unembed, targets):
    logits = jnp.dot(token_rows, unembed, preferred_element_type=jnp.float32)
    row_max = jnp.max(logits, axis=1)
    row_total = jnp.sum(jnp.exp(logits - row_max[:, None]), axis=1)
    chosen = jnp.take_along_axis(logits, targets[:, None].astype(jnp.int32), axis=1)[:, 0]
    return row_max + jnp.log(row_total) - chosen


def covariance(train_losses, query_losses):
    train_centered = train_losses - jnp.mean(train_losses, axis=0, keepdims=True)
    query_centered = query_losses - jnp.mean(query_losses, axis=0, keepdims=True)
    draw_count = train_losses.shape[0]
    return jnp.dot(train_centered.T, query_centered, precision=lax.Precision.HIGHEST, preferred_element_type=jnp.float32) / (draw_count - 1.0)


def reference(hidden, unembed, targets):
    losses = lax.map(lambda token_rows: token_losses(token_rows, unembed, targets), hidden)
    return covariance(losses[:, :TRAIN], losses[:, TRAIN:])
```

```python
import jax
import jax.numpy as jnp
from jax import lax
from jax.experimental import pallas as pl
from jax.experimental.pallas import tpu as pltpu
from jax.sharding import Mesh
from jax.sharding import PartitionSpec as P

TRAIN = 256
LANES = 128
WIDTH = 2432
TILES = (512, 512, 512, 512, 384)
CUT = 48


def shift(x, axis, by):
    size = lax.axis_size(axis)
    return lax.ppermute(x, axis, [(i, (i + by) % size) for i in range(size)])


def loss_kernel(
    place_ref, wanted_ref, *refs, pieces, rows_each, row_copies, depth_copies
):
    inputs = refs[:pieces]
    out_ref, held, weights, top, total, picked, sems = refs[pieces:]
    copies = []
    for k, (slot, size) in enumerate(depth_copies + row_copies):
        target = weights if k < len(depth_copies) else held
        start = pl.multiple_of(place_ref[k], 16)
        copies.append(
            pltpu.make_async_copy(
                inputs[k], target.at[pl.ds(start, size), :], sems.at[k]
            )
        )
    for copy in copies:
        copy.start()
    for copy in copies:
        copy.wait()
    limit = place_ref[len(copies)]
    blocks = held.shape[0] // rows_each

    def one_block(block, carry):
        rows = held[pl.ds(pl.multiple_of(block * rows_each, 16), rows_each), :]
        wanted = wanted_ref[...]
        at = 0
        for step, width in enumerate(TILES):
            tile = jnp.dot(
                rows,
                weights[:, at : at + width],
                preferred_element_type=jnp.float32,
            )
            parts = []
            for g in range(0, width, LANES):
                part = tile[:, g : g + LANES]
                chosen = jnp.where(
                    wanted == at + g, part, 0.0 if at + g == 0 else picked[...]
                )
                picked[...] = chosen
                if at + g + LANES > WIDTH - 256:
                    lane = lax.broadcasted_iota(jnp.int32, part.shape, 1)
                    part = jnp.where(lane + (at + g) < limit, part, -jnp.inf)
                parts.append(part)
            high = parts[0]
            for part in parts[1:]:
                high = jnp.maximum(high, part)
            if step:
                before = top[...]
                high = jnp.maximum(high, before)
                summed = total[...] * jnp.exp(before - high)
            else:
                summed = 0.0
            for part in parts:
                summed = summed + jnp.exp(part - high)
            top[...] = high
            total[...] = summed
            at += width
        top_t = jnp.transpose(top[...])
        total_t = jnp.transpose(total[...])
        picked_t = jnp.transpose(picked[...])
        high = jnp.max(top_t, axis=0, keepdims=True)
        summed = jnp.sum(total_t * jnp.exp(top_t - high), axis=0, keepdims=True)
        out_ref[0, pl.ds(block, 1), :] = high + jnp.log(summed)
        out_ref[1, pl.ds(block, 1), :] = jnp.sum(picked_t, axis=0, keepdims=True)
        return carry

    lax.fori_loop(0, blocks, one_block, 0)


def local_stats(depth_pieces, row_pieces, wanted, limit, rows_each, row_total):
    width = depth_pieces[0][0].shape[-1]
    depth = row_pieces[0][0].shape[-1]
    depth_copies = tuple((k, a.shape[0]) for k, (a, _) in enumerate(depth_pieces))
    row_copies = tuple((k, a.shape[0]) for k, (a, _) in enumerate(row_pieces))
    everything = list(depth_pieces) + list(row_pieces)
    place = jnp.stack([jnp.asarray(s, jnp.int32) for _, s in everything] + [limit])
    pieces = [a for a, _ in everything]
    blocks = row_total // rows_each

    def kernel(*refs):
        loss_kernel(
            *refs,
            pieces=len(pieces),
            rows_each=rows_each,
            row_copies=row_copies,
            depth_copies=depth_copies,
        )

    return pl.pallas_call(
        kernel,
        out_shape=jax.ShapeDtypeStruct((2, blocks, rows_each), jnp.float32),
        in_specs=[
            pl.BlockSpec(memory_space=pltpu.SMEM),
            pl.BlockSpec(memory_space=pltpu.VMEM),
        ]
        + [pl.BlockSpec(memory_space=pl.ANY)] * len(pieces),
        out_specs=pl.BlockSpec(memory_space=pltpu.VMEM),
        scratch_shapes=[
            pltpu.VMEM((row_total, depth), jnp.bfloat16),
            pltpu.VMEM((depth, width), jnp.bfloat16),
            pltpu.VMEM((rows_each, LANES), jnp.float32),
            pltpu.VMEM((rows_each, LANES), jnp.float32),
            pltpu.VMEM((rows_each, LANES), jnp.float32),
            pltpu.SemaphoreType.DMA((len(pieces),)),
        ],
        compiler_params=pltpu.CompilerParams(vmem_limit_bytes=40 * 2**20),
        cost_estimate=pl.CostEstimate(
            flops=2 * row_total * depth * width,
            bytes_accessed=2 * depth * (row_total + width),
            transcendentals=row_total * width,
        ),
    )(place, wanted, *pieces)


def covariance(train_losses, query_losses):
    train_centered = train_losses - jnp.mean(train_losses, axis=0, keepdims=True)
    query_centered = query_losses - jnp.mean(query_losses, axis=0, keepdims=True)
    draw_count = train_losses.shape[0]
    return jnp.dot(
        train_centered.T,
        query_centered,
        precision=lax.Precision.HIGHEST,
        preferred_element_type=jnp.float32,
    ) / (draw_count - 1.0)


def body(hidden, unembed, targets):
    draws, tokens, model_width = hidden.shape
    depth_each, columns = unembed.shape
    nx, nz = lax.axis_size("x"), lax.axis_size("z")
    ny, nc = lax.axis_size("y"), lax.axis_size("c")
    x, z, y, c = (lax.axis_index(name) for name in ("x", "z", "y", "c"))

    padded = jnp.pad(unembed, ((0, 0), (0, nx * WIDTH - columns)))
    blocks = jnp.stack([padded[:, k * WIDTH : (k + 1) * WIDTH] for k in range(nx)])
    own = lax.all_to_all(blocks, "x", 0, 0, tiled=True)
    own = own.reshape(nx * depth_each, WIDTH)
    span = nx * depth_each
    depth_pieces = [(own, z * span)]
    up = down = own
    for k in range(1, nz // 2):
        up, down = shift(up, "z", 1), shift(down, "z", -1)
        depth_pieces.append((up, (z + nz - k) % nz * span))
        depth_pieces.append((down, (z + k) % nz * span))
    far = (z + nz // 2) % nz * span
    depth_pieces.append((shift(up[:CUT], "z", 1), far))
    depth_pieces.append((shift(down[CUT:], "z", -1), far + CUT))

    source = jnp.arange(model_width, dtype=jnp.int32)
    zp, rest = source // span, source % span
    source = (rest // depth_each * nz + zp) * depth_each + rest % depth_each
    chooser = (
        lax.broadcasted_iota(jnp.int32, (model_width, model_width), 0)
        == source[None, :]
    ).astype(jnp.bfloat16)
    ordered = jnp.dot(
        hidden.reshape(draws * tokens, model_width),
        chooser,
        preferred_element_type=jnp.float32,
    ).astype(jnp.bfloat16)
    mine = lax.dynamic_slice_in_dim(ordered, c * tokens, tokens, 0)
    half = tokens // 2
    left, right = shift(mine, "x", 1), shift(mine, "x", -1)
    far_left, far_right = shift(left[:half], "x", 1), shift(right[half:], "x", -1)
    near = [
        (left, (x + nx - 1) % nx, 0),
        (right, (x + 1) % nx, 0),
        (far_left, (x + 2) % nx, 0),
        (far_right, (x + 2) % nx, half),
    ]
    row_pieces = [(ordered, x * draws * tokens)]
    for rows, at, extra in near:
        row_pieces.append((rows, (at * draws + c) * tokens + extra))
        row_pieces.append((shift(rows, "c", 1), (at * draws + 1 - c) * tokens + extra))

    first_column = (y * nc + c) * columns + x * WIDTH
    wanted = (
        targets[:, None]
        - first_column
        - lax.broadcasted_iota(jnp.int32, (tokens, LANES), 1)
    )
    limit = jnp.minimum(columns - x * WIDTH, WIDTH).astype(jnp.int32)
    stats = local_stats(
        depth_pieces, row_pieces, wanted, limit, tokens, nx * draws * tokens
    )

    part = TRAIN // nx
    sent = jnp.stack(
        [
            jnp.concatenate(
                [stats[:, :, k * part : (k + 1) * part], stats[:, :, TRAIN:]], axis=-1
            )
            for k in range(nx)
        ]
    )
    sent = jnp.broadcast_to(sent[:, None], (nx, ny * nc, *sent.shape[1:]))
    sent = sent.reshape(nx * ny * nc, *sent.shape[2:])
    got = lax.all_to_all(sent, ("x", "y", "c"), 0, 0, tiled=True)
    high = jnp.max(got[:, 0], axis=0)
    losses = (
        high
        + jnp.log(jnp.sum(jnp.exp(got[:, 0] - high[None]), axis=0))
        - jnp.sum(got[:, 1], axis=0)
    )
    each = part // nz
    sent = jnp.stack(
        [
            jnp.concatenate([losses[:, k * each : (k + 1) * each], losses[:, part:]], -1)
            for k in range(nz)
        ]
    )
    got = lax.all_to_all(sent, "z", 0, 0, tiled=True)
    got = got.reshape(-1, got.shape[-1])
    return covariance(got[:, :each], got[:, each:])


def solution(mesh):
    split = Mesh(mesh.devices.reshape(4, 8, 4, 2), ("x", "z", "y", "c"))
    draw, vocab = ("x", "z"), ("y", "c")
    placed = (P(draw, None, None), P(draw, vocab), P())
    return jax.shard_map(
        body, mesh=split, in_specs=placed, out_specs=P(draw, None), check_vma=False
    )
```

```python
import functools

import jax
import jax.numpy as jnp
from jax import lax
from jax.experimental import pallas as pl
from jax.experimental.pallas import tpu as pltpu
from jax.sharding import Mesh
from jax.sharding import PartitionSpec as P

TRAIN = 256
LANES = 128
WIDTHS = (1280, 1152)
WIDTH = sum(WIDTHS)
WIDEST = 512
CHUNK = 32


def shift(x, axis, by):
    size = lax.axis_size(axis)
    return lax.ppermute(x, axis, [(i, (i + by) % size) for i in range(size)])


def loss_kernel(place_ref, wanted_ref, *refs, sizes, counts, masked, merged):
    pieces = len(sizes)
    earlier_ref = refs[0] if merged else None
    refs = refs[1:] if merged else refs
    inputs = refs[:pieces]
    out_ref, held, weights, logits, top, total, picked, sems = refs[pieces:]
    tokens = wanted_ref.shape[0]
    rows_each = top.shape[0]
    blocks = held.shape[0] // rows_each
    copies, groups = [], []
    for count in counts:
        groups.append(range(len(copies), len(copies) + count))
        for k in groups[-1]:
            target = held if len(groups) > 1 else weights
            start = pl.multiple_of(place_ref[k], 16)
            copies.append(
                pltpu.make_async_copy(
                    inputs[k], target.at[pl.ds(start, sizes[k]), :], sems.at[k]
                )
            )
    for copy in copies:
        copy.start()
    limit = place_ref[pieces]
    width_all = weights.shape[1]
    tiles = [min(WIDEST, width_all - at) for at in range(0, width_all, WIDEST)]

    def product(slot, block, at, width):
        rows = held[pl.ds(pl.multiple_of(block * rows_each, 16), rows_each), :]
        logits[slot, :, :width] = jnp.dot(
            rows, weights[:, at : at + width], preferred_element_type=jnp.float32
        )

    def absorb(slot, at, width):
        for r in range(0, rows_each, CHUNK):
            some = slice(r, r + CHUNK)
            wanted = wanted_ref[r % tokens : r % tokens + CHUNK, :]
            chosen = picked[some, :] if at else jnp.zeros((CHUNK, LANES), jnp.float32)
            parts = []
            for g in range(0, width, LANES):
                part = logits[slot, some, g : g + LANES]
                chosen = jnp.where(wanted == at + g, part, chosen)
                if at + g >= width_all - masked:
                    lane = lax.broadcasted_iota(jnp.int32, part.shape, 1)
                    part = jnp.where(lane + (at + g) < limit, part, -jnp.inf)
                parts.append(part)
            high = parts[0]
            for part in parts[1:]:
                high = jnp.maximum(high, part)
            summed = jnp.zeros((CHUNK, LANES), jnp.float32)
            if at:
                before = top[some, :]
                high = jnp.maximum(high, before)
                summed = total[some, :] * jnp.exp(before - high)
            for part in parts:
                summed = summed + jnp.exp(part - high)
            top[some, :] = high
            total[some, :] = summed
            picked[some, :] = chosen

    def finish(block):
        for r in range(0, rows_each, LANES):
            some = slice(r, r + LANES)
            tops = jnp.transpose(top[some, :])
            totals = jnp.transpose(total[some, :])
            chosen = jnp.transpose(picked[some, :])
            high = jnp.max(tops, axis=0, keepdims=True)
            summed = jnp.sum(totals * jnp.exp(tops - high), axis=0, keepdims=True)
            chosen = jnp.sum(chosen, axis=0, keepdims=True)
            row = place_ref[pieces + 1 + block] + r // tokens
            at = slice(r % tokens, r % tokens + LANES)
            if merged:
                before = earlier_ref[0, row, :, at]
                joined = jnp.maximum(before, high)
                summed = summed * jnp.exp(high - joined) + jnp.exp(before - joined)
                high = joined
                chosen = chosen + earlier_ref[1, row, :, at]
            out_ref[0, row, :, at] = high + jnp.log(summed)
            out_ref[1, row, :, at] = chosen

    starts = [sum(tiles[:k]) for k in range(len(tiles))]
    last = (2, starts[-1], tiles[-1])

    def one_block(block, carry):
        for k, group in enumerate(groups[1:]):

            @pl.when(block == k)
            def _():
                for n in group:
                    copies[n].wait()

        product(0, block, starts[0], tiles[0])
        absorb(*last)
        finish(jnp.maximum(block - 1, 0))
        for step in range(1, len(tiles)):
            slot = 2 if step == len(tiles) - 1 else step % 2
            product(slot, block, starts[step], tiles[step])
            absorb((step - 1) % 2, starts[step - 1], tiles[step - 1])
        return carry

    for n in groups[0]:
        copies[n].wait()
    lax.fori_loop(0, blocks, one_block, 0)
    absorb(*last)
    finish(blocks - 1)


def local_stats(depth_pieces, row_blocks, spots, wanted, limit, masked, earlier=()):
    width = depth_pieces[0][0].shape[-1]
    depth = row_blocks[0][0][0].shape[-1]
    rows_each = sum(a.shape[0] for a, _ in row_blocks[0])
    blocks = len(row_blocks)
    groups = [list(depth_pieces)] + [
        [(a, k * rows_each + at) for a, at in block]
        for k, block in enumerate(row_blocks)
    ]
    everything = [piece for group in groups for piece in group]
    place = jnp.stack([jnp.asarray(s, jnp.int32) for _, s in everything] + [limit] + spots)
    pieces = [a for a, _ in everything]
    sizes = tuple(a.shape[0] for a in pieces)
    counts = tuple(len(group) for group in groups)
    state = pltpu.VMEM((rows_each, LANES), jnp.float32)
    return pl.pallas_call(
        functools.partial(
            loss_kernel, sizes=sizes, counts=counts, masked=masked, merged=len(earlier)
        ),
        out_shape=jax.ShapeDtypeStruct(
            (2, blocks * rows_each // wanted.shape[0], 1, wanted.shape[0]), jnp.float32
        ),
        in_specs=[
            pl.BlockSpec(memory_space=pltpu.SMEM),
            pl.BlockSpec(memory_space=pltpu.VMEM),
        ]
        + [pl.BlockSpec(memory_space=pltpu.VMEM)] * len(earlier)
        + [pl.BlockSpec(memory_space=pl.ANY)] * len(pieces),
        out_specs=pl.BlockSpec(memory_space=pltpu.VMEM),
        scratch_shapes=[
            pltpu.VMEM((blocks * rows_each, depth), jnp.bfloat16),
            pltpu.VMEM((depth, width), jnp.bfloat16),
            pltpu.VMEM((3, rows_each, WIDEST), jnp.float32),
            state,
            state,
            state,
            pltpu.SemaphoreType.DMA((len(pieces),)),
        ],
        compiler_params=pltpu.CompilerParams(vmem_limit_bytes=40 * 2**20),
        cost_estimate=pl.CostEstimate(
            flops=2 * blocks * rows_each * depth * width,
            bytes_accessed=2 * depth * (blocks * rows_each + width),
            transcendentals=blocks * rows_each * width,
        ),
    )(place, wanted, *earlier, *pieces)


def covariance(train_losses, query_losses):
    train_centered = train_losses - jnp.mean(train_losses, axis=0, keepdims=True)
    query_centered = query_losses - jnp.mean(query_losses, axis=0, keepdims=True)
    draw_count = train_losses.shape[0]
    return jnp.dot(
        train_centered.T,
        query_centered,
        precision=lax.Precision.HIGHEST,
        preferred_element_type=jnp.float32,
    ) / (draw_count - 1.0)


def body(hidden, unembed, targets):
    draws, tokens, model_width = hidden.shape
    depth_each, columns = unembed.shape
    nx, nz = lax.axis_size("x"), lax.axis_size("z")
    ny, nc = lax.axis_size("y"), lax.axis_size("c")
    x, z, y, c = (lax.axis_index(name) for name in ("x", "z", "y", "c"))

    padded = jnp.pad(unembed, ((0, 0), (0, nx * WIDTH - columns)))
    blocks = jnp.stack([padded[:, k * WIDTH : (k + 1) * WIDTH] for k in range(nx)])
    own = lax.all_to_all(blocks, "x", 0, 0, tiled=True)
    span = nx * depth_each
    depth_pieces = []
    for half, (at, width) in enumerate(((0, WIDTHS[0]), (WIDTHS[0], WIDTHS[1]))):
        part = own[:, :, at : at + width].reshape(span, width)
        found = [(part, z * span)]
        up = down = part
        for k in range(1, nz // 2):
            up = shift(up, "z", 1)
            down = shift(down, "z", -1)
            found.append((up, (z + nz - k) % nz * span))
            found.append((down, (z + k) % nz * span))
        far = (up, 1) if not half else (down, -1)
        far = shift(far[0], "z", far[1])
        found.append((far, (z + nz // 2) % nz * span))
        depth_pieces.append(found)

    source = jnp.arange(model_width, dtype=jnp.int32)
    zp, rest = source // span, source % span
    source = (rest // depth_each * nz + zp) * depth_each + rest % depth_each
    chooser = (
        lax.broadcasted_iota(jnp.int32, (model_width, model_width), 0)
        == source[None, :]
    ).astype(jnp.bfloat16)
    ordered = jnp.dot(
        hidden.reshape(draws * tokens, model_width),
        chooser,
        preferred_element_type=jnp.float32,
    ).astype(jnp.bfloat16)
    mine = lax.dynamic_slice_in_dim(ordered, c * tokens, tokens, 0)
    mine, _ = lax.optimization_barrier((mine, own))
    left, right = shift(mine, "x", 1), shift(mine, "x", -1)
    row_blocks = [[(ordered, 0)]]
    for rows in (left, right, shift(left, "x", 1)):
        row_blocks.append([(rows, c * tokens), (shift(rows, "c", 1), (1 - c) * tokens)])
    spots = [(x + k) % nx * draws for k in (0, nx - 1, 1, 2)]

    first_column = (y * nc + c) * columns + x * WIDTH
    wanted = (
        targets[:, None]
        - first_column
        - lax.broadcasted_iota(jnp.int32, (tokens, LANES), 1)
    )
    limit = jnp.minimum(columns - x * WIDTH, WIDTH).astype(jnp.int32)
    first = local_stats(depth_pieces[0], row_blocks, spots, wanted, limit, 0)
    stats = local_stats(
        depth_pieces[1],
        row_blocks,
        spots,
        wanted - WIDTHS[0],
        limit - WIDTHS[0],
        256,
        (first,),
    )[:, :, 0]

    sent = jnp.stack(
        [
            jnp.concatenate([stats[:, :, at : at + LANES], stats[:, :, TRAIN:]], axis=-1)
            for at in range(0, TRAIN, LANES)
        ]
    )
    sent = jnp.broadcast_to(
        sent[:, None], (len(sent), nx // len(sent) * ny * nc, *sent.shape[1:])
    )
    sent = sent.reshape(nx * ny * nc, *sent.shape[2:])
    got = lax.all_to_all(sent, ("x", "y", "c"), 0, 0, tiled=True)
    high = jnp.max(got[:, 0], axis=0)
    losses = (
        high
        + jnp.log(jnp.sum(jnp.exp(got[:, 0] - high[None]), axis=0))
        - jnp.sum(got[:, 1], axis=0)
    )
    got = lax.all_to_all(
        jnp.broadcast_to(losses[None], (nz, *losses.shape)), "z", 0, 0, tiled=True
    )
    got = got.reshape(-1, got.shape[-1])
    each = TRAIN // (nx * nz)
    mine = lax.dynamic_slice_in_dim(got, (x * nz + z) * each % LANES, each, 1)
    return covariance(mine, got[:, LANES:])


def solution(mesh):
    split = Mesh(mesh.devices.reshape(4, 8, 4, 2), ("x", "z", "y", "c"))
    draw, vocab = ("x", "z"), ("y", "c")
    placed = (P(draw, None, None), P(draw, vocab), P())
    return jax.shard_map(
        body, mesh=split, in_specs=placed, out_specs=P(draw, None), check_vma=False
    )
```

```python
import functools

import jax
import jax.numpy as jnp
from jax import lax
from jax.experimental import pallas as pl
from jax.experimental.pallas import tpu as pltpu
from jax.sharding import Mesh
from jax.sharding import PartitionSpec as P

TRAIN = 256
LANES = 128
WIDTHS = (1280, 1152)
WIDTH = sum(WIDTHS)
WIDEST = 512
CHUNK = 32


def shift(x, axis, by):
    size = lax.axis_size(axis)
    return lax.ppermute(x, axis, [(i, (i + by) % size) for i in range(size)])


def loss_kernel(place_ref, wanted_ref, *refs, sizes, counts, masked, merged):
    pieces = len(sizes)
    earlier_ref = refs[0] if merged else None
    refs = refs[1:] if merged else refs
    inputs = refs[:pieces]
    out_ref, held, weights, logits, top, total, picked, sems = refs[pieces:]
    tokens = wanted_ref.shape[0]
    rows_each = top.shape[0]
    blocks = held.shape[0] // rows_each
    copies, groups = [], []
    for count in counts:
        groups.append(range(len(copies), len(copies) + count))
        for k in groups[-1]:
            target = held if len(groups) > 1 else weights
            start = pl.multiple_of(place_ref[k], 16)
            copies.append(
                pltpu.make_async_copy(
                    inputs[k], target.at[pl.ds(start, sizes[k]), :], sems.at[k]
                )
            )
    for copy in copies:
        copy.start()
    limit = place_ref[pieces]
    width_all = weights.shape[1]
    tiles = [min(WIDEST, width_all - at) for at in range(0, width_all, WIDEST)]

    def product(slot, block, at, width):
        rows = held[pl.ds(pl.multiple_of(block * rows_each, 16), rows_each), :]
        logits[slot, :, :width] = jnp.dot(
            rows, weights[:, at : at + width], preferred_element_type=jnp.float32
        )

    def absorb(slot, at, width):
        for r in range(0, rows_each, CHUNK):
            some = slice(r, r + CHUNK)
            wanted = wanted_ref[r % tokens : r % tokens + CHUNK, :]
            chosen = picked[some, :] if at else jnp.zeros((CHUNK, LANES), jnp.float32)
            parts = []
            for g in range(0, width, LANES):
                part = logits[slot, some, g : g + LANES]
                chosen = jnp.where(wanted == at + g, part, chosen)
                if at + g >= width_all - masked:
                    lane = lax.broadcasted_iota(jnp.int32, part.shape, 1)
                    part = jnp.where(lane + (at + g) < limit, part, -jnp.inf)
                parts.append(part)
            high = parts[0]
            for part in parts[1:]:
                high = jnp.maximum(high, part)
            summed = jnp.zeros((CHUNK, LANES), jnp.float32)
            if at:
                before = top[some, :]
                high = jnp.maximum(high, before)
                summed = total[some, :] * jnp.exp(before - high)
            for part in parts:
                summed = summed + jnp.exp(part - high)
            top[some, :] = high
            total[some, :] = summed
            picked[some, :] = chosen

    def finish(block):
        for r in range(0, rows_each, LANES):
            some = slice(r, r + LANES)
            lane = lax.broadcasted_iota(jnp.int32, (LANES, LANES), 1)
            high = jnp.max(top[some, :], axis=1, keepdims=True)
            summed = total[some, :] * jnp.exp(top[some, :] - high)
            summed = jnp.sum(summed, axis=1, keepdims=True)
            chosen = jnp.sum(picked[some, :], axis=1, keepdims=True)
            both = jnp.transpose(jnp.where(lane == 0, high + jnp.log(summed), chosen))
            high, chosen = both[0:1, :], both[1:2, :]
            row = place_ref[pieces + 1 + block] + r // tokens
            at = slice(r % tokens, r % tokens + LANES)
            if merged:
                before = earlier_ref[row, :, at]
                joined = jnp.maximum(before, high)
                high = joined + jnp.log(
                    jnp.exp(high - joined) + jnp.exp(before - joined)
                )
                chosen = chosen + earlier_ref[row + 4, :, at]
            out_ref[row, :, at] = high
            out_ref[row + 4, :, at] = chosen

    starts = [sum(tiles[:k]) for k in range(len(tiles))]
    last = (2, starts[-1], tiles[-1])

    def one_block(block, carry):
        for k, group in enumerate(groups[1:]):

            @pl.when(block == k)
            def _():
                for n in group:
                    copies[n].wait()

        product(0, block, starts[0], tiles[0])
        absorb(*last)
        finish(jnp.maximum(block - 1, 0))
        for step in range(1, len(tiles)):
            slot = 2 if step == len(tiles) - 1 else step % 2
            product(slot, block, starts[step], tiles[step])
            absorb((step - 1) % 2, starts[step - 1], tiles[step - 1])
        return carry

    for n in groups[0]:
        copies[n].wait()
    lax.fori_loop(0, blocks, one_block, 0)
    absorb(*last)
    finish(blocks - 1)


def local_stats(depth_pieces, row_blocks, spots, wanted, limit, masked, earlier=()):
    width = depth_pieces[0][0].shape[-1]
    depth = row_blocks[0][0][0].shape[-1]
    rows_each = sum(a.shape[0] for a, _ in row_blocks[0])
    blocks = len(row_blocks)
    groups = [list(depth_pieces)] + [
        [(a, k * rows_each + at) for a, at in block]
        for k, block in enumerate(row_blocks)
    ]
    everything = [piece for group in groups for piece in group]
    place = jnp.stack([jnp.asarray(s, jnp.int32) for _, s in everything] + [limit] + spots)
    pieces = [a for a, _ in everything]
    sizes = tuple(a.shape[0] for a in pieces)
    counts = tuple(len(group) for group in groups)
    state = pltpu.VMEM((rows_each, LANES), jnp.float32)
    return pl.pallas_call(
        functools.partial(
            loss_kernel, sizes=sizes, counts=counts, masked=masked, merged=len(earlier)
        ),
        out_shape=jax.ShapeDtypeStruct(
            (2 * blocks * rows_each // wanted.shape[0], 1, wanted.shape[0]), jnp.float32
        ),
        in_specs=[
            pl.BlockSpec(memory_space=pltpu.SMEM),
            pl.BlockSpec(memory_space=pltpu.VMEM),
        ]
        + [pl.BlockSpec(memory_space=pltpu.VMEM)] * len(earlier)
        + [pl.BlockSpec(memory_space=pl.ANY)] * len(pieces),
        out_specs=pl.BlockSpec(memory_space=pltpu.VMEM),
        scratch_shapes=[
            pltpu.VMEM((blocks * rows_each, depth), jnp.bfloat16),
            pltpu.VMEM((depth, width), jnp.bfloat16),
            pltpu.VMEM((3, rows_each, WIDEST), jnp.float32),
            state,
            state,
            state,
            pltpu.SemaphoreType.DMA((len(pieces),)),
        ],
        compiler_params=pltpu.CompilerParams(vmem_limit_bytes=40 * 2**20),
        cost_estimate=pl.CostEstimate(
            flops=2 * blocks * rows_each * depth * width,
            bytes_accessed=2 * depth * (blocks * rows_each + width),
            transcendentals=blocks * rows_each * width,
        ),
    )(place, wanted, *earlier, *pieces)


def covariance(train_losses, query_losses):
    train_centered = train_losses - jnp.mean(train_losses, axis=0, keepdims=True)
    query_centered = query_losses - jnp.mean(query_losses, axis=0, keepdims=True)
    draw_count = train_losses.shape[0]
    return jnp.dot(
        train_centered.T,
        query_centered,
        precision=lax.Precision.HIGHEST,
        preferred_element_type=jnp.float32,
    ) / (draw_count - 1.0)


def body(hidden, unembed, targets):
    draws, tokens, model_width = hidden.shape
    depth_each, columns = unembed.shape
    nx, nz = lax.axis_size("x"), lax.axis_size("z")
    ny, nc = lax.axis_size("y"), lax.axis_size("c")
    x, z, y, c = (lax.axis_index(name) for name in ("x", "z", "y", "c"))

    padded = jnp.pad(unembed, ((0, 0), (0, nx * WIDTH - columns)))
    blocks = jnp.stack([padded[:, k * WIDTH : (k + 1) * WIDTH] for k in range(nx)])
    own = lax.all_to_all(blocks, "x", 0, 0, tiled=True)
    span = nx * depth_each
    depth_pieces = []
    for half, (at, width) in enumerate(((0, WIDTHS[0]), (WIDTHS[0], WIDTHS[1]))):
        part = own[:, :, at : at + width].reshape(span, width)
        found = [(part, z * span)]
        up = down = part
        for k in range(1, nz // 2):
            up = shift(up, "z", 1)
            down = shift(down, "z", -1)
            found.append((up, (z + nz - k) % nz * span))
            found.append((down, (z + k) % nz * span))
        far = (up, 1) if not half else (down, -1)
        far = shift(far[0], "z", far[1])
        found.append((far, (z + nz // 2) % nz * span))
        depth_pieces.append(found)

    source = jnp.arange(model_width, dtype=jnp.int32)
    zp, rest = source // span, source % span
    source = (rest // depth_each * nz + zp) * depth_each + rest % depth_each
    chooser = (
        lax.broadcasted_iota(jnp.int32, (model_width, model_width), 0)
        == source[None, :]
    ).astype(jnp.bfloat16)
    ordered = jnp.dot(
        hidden.reshape(draws * tokens, model_width),
        chooser,
        preferred_element_type=jnp.float32,
    ).astype(jnp.bfloat16)
    mine = lax.dynamic_slice_in_dim(ordered, c * tokens, tokens, 0)
    mine, _ = lax.optimization_barrier((mine, own))
    left, right = shift(mine, "x", 1), shift(mine, "x", -1)
    row_blocks = [[(ordered, 0)]]
    for rows in (left, right, shift(left, "x", 1)):
        row_blocks.append([(rows, c * tokens), (shift(rows, "c", 1), (1 - c) * tokens)])
    spots = [(x + k) % nx for k in (0, nx - 1, 1, 2)]
    spots = [at // nc * (4 * draws) + at % nc * draws for at in spots]

    first_column = (y * nc + c) * columns + x * WIDTH
    wanted = (
        targets[:, None]
        - first_column
        - lax.broadcasted_iota(jnp.int32, (tokens, LANES), 1)
    )
    limit = jnp.minimum(columns - x * WIDTH, WIDTH).astype(jnp.int32)
    first = local_stats(depth_pieces[0], row_blocks, spots, wanted, limit, 0)
    stats = local_stats(
        depth_pieces[1],
        row_blocks,
        spots,
        wanted - WIDTHS[0],
        limit - WIDTHS[0],
        256,
        (first,),
    ).reshape(nc, 4 * draws, tokens)

    sent = jnp.stack(
        [
            jnp.concatenate([stats[:, :, at : at + LANES], stats[:, :, TRAIN:]], axis=-1)
            for at in range(0, TRAIN, LANES)
        ]
    )
    sent = jnp.broadcast_to(
        sent[:, None], (len(sent), nx // len(sent) * ny, *sent.shape[1:])
    )
    sent = sent.reshape(nx * ny * nc, *sent.shape[3:])
    got = lax.all_to_all(sent, ("x", "y", "c"), 0, 0, tiled=True)
    logs, chosen = got[:, : 2 * draws], got[:, 2 * draws :]
    high = jnp.max(logs, axis=0)
    losses = (
        high
        + jnp.log(jnp.sum(jnp.exp(logs - high[None]), axis=0))
        - jnp.sum(chosen, axis=0)
    )
    got = lax.all_to_all(
        jnp.broadcast_to(losses[None], (nz * nc, *losses.shape)),
        ("z", "c"),
        0,
        0,
        tiled=True,
    )
    got = got.reshape(-1, got.shape[-1])
    each = TRAIN // (nx * nz)
    mine = lax.dynamic_slice_in_dim(got, (x * nz + z) * each % LANES, each, 1)
    return covariance(mine, got[:, LANES:])


def solution(mesh):
    split = Mesh(mesh.devices.reshape(4, 8, 4, 2), ("x", "z", "y", "c"))
    draw, vocab = ("x", "z"), ("y", "c")
    placed = (P(draw, None, None), P(draw, vocab), P())
    return jax.shard_map(
        body, mesh=split, in_specs=placed, out_specs=P(draw, None), check_vma=False
    )
```

```python
import functools

import jax
import jax.numpy as jnp
from jax import lax
from jax.experimental import pallas as pl
from jax.experimental.pallas import tpu as pltpu
from jax.sharding import Mesh
from jax.sharding import PartitionSpec as P

TRAIN = 256
LANES = 128
WIDTHS = (1280, 1152)
WIDTH = sum(WIDTHS)
WIDEST = 512
CHUNK = 32


def shift(x, axis, by):
    size = lax.axis_size(axis)
    return lax.ppermute(x, axis, [(i, (i + by) % size) for i in range(size)])


def loss_kernel(place_ref, wanted_ref, *refs, sizes, counts):
    pieces = len(sizes)
    inputs = refs[:pieces]
    out_ref, held, weights, logits, top, total, picked, sems = refs[pieces:]
    tokens = wanted_ref.shape[0]
    rows_each = top.shape[0]
    blocks = held.shape[0] // rows_each
    width_all = weights.shape[1]
    tiles = [min(WIDEST, width_all - at) for at in range(0, width_all, WIDEST)]
    starts = [sum(tiles[:k]) for k in range(len(tiles))]

    tile_copies, block_copies = [[]], []
    used = 0
    for k in range(counts[0]):
        lo = 0 if inputs[k].shape[1] == WIDTHS[0] else WIDTHS[0]
        rows = pl.ds(pl.multiple_of(place_ref[k], 16), sizes[k])
        piece = weights.at[rows, lo : lo + inputs[k].shape[1]]
        tile_copies[0].append(pltpu.make_async_copy(inputs[k], piece, sems.at[used]))
        used += 1
    k = counts[0]
    for count in counts[1:]:
        block_copies.append([])
        for _ in range(count):
            rows = pl.ds(pl.multiple_of(place_ref[k], 16), sizes[k])
            block_copies[-1].append(
                pltpu.make_async_copy(inputs[k], held.at[rows, :], sems.at[used])
            )
            used, k = used + 1, k + 1
    order = [*tile_copies, *block_copies]
    for group in order:
        for copy in group:
            copy.start()
    limit = place_ref[pieces]

    def product(slot, block, at, width):
        rows = held[pl.ds(pl.multiple_of(block * rows_each, 16), rows_each), :]
        logits[slot, :, :width] = jnp.dot(
            rows, weights[:, at : at + width], preferred_element_type=jnp.float32
        )

    def absorb(slot, at, width):
        for r in range(0, rows_each, CHUNK):
            some = slice(r, r + CHUNK)
            wanted = wanted_ref[r % tokens : r % tokens + CHUNK, :]
            chosen = picked[some, :] if at else jnp.zeros((CHUNK, LANES), jnp.float32)
            parts = []
            for g in range(0, width, LANES):
                part = logits[slot, some, g : g + LANES]
                chosen = jnp.where(wanted == at + g, part, chosen)
                if at + g >= width_all - 2 * LANES:
                    lane = lax.broadcasted_iota(jnp.int32, part.shape, 1)
                    part = jnp.where(lane + (at + g) < limit, part, -jnp.inf)
                parts.append(part)
            high = parts[0]
            for part in parts[1:]:
                high = jnp.maximum(high, part)
            summed = jnp.zeros((CHUNK, LANES), jnp.float32)
            if at:
                before = top[some, :]
                high = jnp.maximum(high, before)
                summed = total[some, :] * jnp.exp(before - high)
            for part in parts:
                summed = summed + jnp.exp(part - high)
            top[some, :] = high
            total[some, :] = summed
            picked[some, :] = chosen

    def finish(block):
        for r in range(0, rows_each, LANES):
            some = slice(r, r + LANES)
            lane = lax.broadcasted_iota(jnp.int32, (LANES, LANES), 1)
            high = jnp.max(top[some, :], axis=1, keepdims=True)
            summed = total[some, :] * jnp.exp(top[some, :] - high)
            summed = jnp.sum(summed, axis=1, keepdims=True)
            chosen = jnp.sum(picked[some, :], axis=1, keepdims=True)
            both = jnp.transpose(jnp.where(lane == 0, high + jnp.log(summed), chosen))
            high, chosen = both[0:1, :], both[1:2, :]
            row = place_ref[pieces + 1 + block] + r // tokens
            at = slice(r % tokens, r % tokens + LANES)
            out_ref[row, :, at] = high
            out_ref[row + 4, :, at] = chosen

    last = (2, starts[-1], tiles[-1])

    def one_block(block, carry):
        def wait(at_block, group):
            @pl.when(block == at_block)
            def _():
                for copy in group:
                    copy.wait()

        for k, group in enumerate(block_copies):
            wait(k, group)
        product(0, block, starts[0], tiles[0])
        absorb(*last)
        finish(jnp.maximum(block - 1, 0))
        for step in range(1, len(tiles)):
            slot = 2 if step == len(tiles) - 1 else step % 2
            product(slot, block, starts[step], tiles[step])
            absorb((step - 1) % 2, starts[step - 1], tiles[step - 1])
        return carry

    for group in tile_copies:
        for copy in group:
            copy.wait()
    lax.fori_loop(0, blocks, one_block, 0)
    absorb(*last)
    finish(blocks - 1)


def join_rows(blocks):
    count, each, _ = blocks.shape
    rows = count * each

    def kernel(in_ref, *out_refs):
        row = lax.broadcasted_iota(jnp.int32, (rows, each), 0)
        column = lax.broadcasted_iota(jnp.int32, (rows, each), 1)
        at = 0
        for out_ref in out_refs:
            size = out_ref.shape[1]
            out_ref[...] = sum(
                jnp.dot(
                    (row == column + k * each).astype(jnp.bfloat16),
                    in_ref[k, :, at : at + size],
                    preferred_element_type=jnp.float32,
                )
                for k in range(count)
            ).astype(jnp.bfloat16)
            at += size

    vmem = pl.BlockSpec(memory_space=pltpu.VMEM)
    return pl.pallas_call(
        kernel,
        out_shape=[jax.ShapeDtypeStruct((rows, w), jnp.bfloat16) for w in WIDTHS],
        in_specs=[vmem],
        out_specs=[vmem] * len(WIDTHS),
    )(blocks)


def join_stats(got, copies):
    half = got.shape[1] // 2

    def kernel(in_ref, out_ref):
        parts = in_ref[...]
        high = jnp.max(parts, axis=0)
        logs = high + jnp.log(jnp.sum(jnp.exp(parts - high[None]), axis=0))
        losses = logs[:half] - jnp.sum(parts, axis=0)[half:]
        for k in range(copies):
            out_ref[k] = losses

    vmem = pl.BlockSpec(memory_space=pltpu.VMEM)
    return pl.pallas_call(
        kernel,
        out_shape=jax.ShapeDtypeStruct((copies, half, got.shape[2]), jnp.float32),
        in_specs=[vmem],
        out_specs=vmem,
    )(got)


def local_stats(depth_pieces, row_blocks, spots, wanted, limit):
    width = WIDTH
    depth = row_blocks[0][0][0].shape[-1]
    rows_each = sum(a.shape[0] for a, _ in row_blocks[0])
    blocks = len(row_blocks)
    groups = [list(depth_pieces)] + [
        [(a, k * rows_each + at) for a, at in block]
        for k, block in enumerate(row_blocks)
    ]
    everything = [piece for group in groups for piece in group]
    place = jnp.stack([jnp.asarray(s, jnp.int32) for _, s in everything] + [limit] + spots)
    pieces = [a for a, _ in everything]
    sizes = tuple(a.shape[0] for a in pieces)
    counts = tuple(len(group) for group in groups)
    state = pltpu.VMEM((rows_each, LANES), jnp.float32)
    return pl.pallas_call(
        functools.partial(loss_kernel, sizes=sizes, counts=counts),
        out_shape=jax.ShapeDtypeStruct(
            (2 * blocks * rows_each // wanted.shape[0], 1, wanted.shape[0]), jnp.float32
        ),
        in_specs=[
            pl.BlockSpec(memory_space=pltpu.SMEM),
            pl.BlockSpec(memory_space=pltpu.VMEM),
        ]
        + [pl.BlockSpec(memory_space=pl.ANY)] * len(pieces),
        out_specs=pl.BlockSpec(memory_space=pltpu.VMEM),
        scratch_shapes=[
            pltpu.VMEM((blocks * rows_each, depth), jnp.bfloat16),
            pltpu.VMEM((depth, width), jnp.bfloat16),
            pltpu.VMEM((3, rows_each, WIDEST), jnp.float32),
            state,
            state,
            state,
            pltpu.SemaphoreType.DMA((len(pieces),)),
        ],
        compiler_params=pltpu.CompilerParams(vmem_limit_bytes=58 * 2**20),
        cost_estimate=pl.CostEstimate(
            flops=2 * blocks * rows_each * depth * width,
            bytes_accessed=2 * depth * (blocks * rows_each + width),
            transcendentals=blocks * rows_each * width,
        ),
    )(place, wanted, *pieces)


def covariance(train_losses, query_losses):
    train_centered = train_losses - jnp.mean(train_losses, axis=0, keepdims=True)
    query_centered = query_losses - jnp.mean(query_losses, axis=0, keepdims=True)
    draw_count = train_losses.shape[0]
    return jnp.dot(
        train_centered.T,
        query_centered,
        precision=lax.Precision.HIGHEST,
        preferred_element_type=jnp.float32,
    ) / (draw_count - 1.0)


def body(hidden, unembed, targets):
    draws, tokens, model_width = hidden.shape
    depth_each, columns = unembed.shape
    nx, nz = lax.axis_size("x"), lax.axis_size("z")
    ny, nc = lax.axis_size("y"), lax.axis_size("c")
    x, z, y, c = (lax.axis_index(name) for name in ("x", "z", "y", "c"))

    padded = jnp.pad(unembed, ((0, 0), (0, nx * WIDTH - columns)))
    blocks = jnp.stack([padded[:, k * WIDTH : (k + 1) * WIDTH] for k in range(nx)])
    own = lax.all_to_all(blocks, "x", 0, 0, tiled=True)
    span = nx * depth_each
    depth_pieces = []
    for half, part in enumerate(join_rows(own)):
        found = [(part, z * span)]
        up = down = part
        for k in range(1, nz // 2):
            up = shift(up, "z", 1)
            down = shift(down, "z", -1)
            found.append((up, (z + nz - k) % nz * span))
            found.append((down, (z + k) % nz * span))
        far = (up, 1) if not half else (down, -1)
        far = shift(far[0], "z", far[1])
        found.append((far, (z + nz // 2) % nz * span))
        depth_pieces.append(found)

    source = jnp.arange(model_width, dtype=jnp.int32)
    zp, rest = source // span, source % span
    source = (rest // depth_each * nz + zp) * depth_each + rest % depth_each
    chooser = (
        lax.broadcasted_iota(jnp.int32, (model_width, model_width), 0)
        == source[None, :]
    ).astype(jnp.bfloat16)
    ordered = jnp.dot(
        hidden.reshape(draws * tokens, model_width),
        chooser,
        preferred_element_type=jnp.float32,
    ).astype(jnp.bfloat16)
    mine = lax.dynamic_slice_in_dim(ordered, c * tokens, tokens, 0)
    each = TRAIN // (nx * nz)
    at = (x * nz + z) * each % LANES
    mine, at, _ = lax.optimization_barrier((mine, at, own))
    left, right = shift(mine, "x", 1), shift(mine, "x", -1)
    row_blocks = [[(ordered, 0)]]
    for rows in (left, right, shift(left, "x", 1)):
        row_blocks.append([(rows, c * tokens), (shift(rows, "c", 1), (1 - c) * tokens)])
    spots = [(x + k) % nx for k in (0, nx - 1, 1, 2)]
    spots = [at // nc * (4 * draws) + at % nc * draws for at in spots]

    first_column = (y * nc + c) * columns + x * WIDTH
    wanted = (
        targets[:, None]
        - first_column
        - lax.broadcasted_iota(jnp.int32, (tokens, LANES), 1)
    )
    limit = jnp.minimum(columns - x * WIDTH, WIDTH).astype(jnp.int32)
    stats = local_stats(
        depth_pieces[0] + depth_pieces[1], row_blocks, spots, wanted, limit
    ).reshape(nc, 4 * draws, tokens)

    sent = jnp.stack(
        [
            jnp.concatenate([stats[:, :, at : at + LANES], stats[:, :, TRAIN:]], axis=-1)
            for at in range(0, TRAIN, LANES)
        ]
    )
    sent = jnp.broadcast_to(
        sent[:, None], (len(sent), nx // len(sent) * ny, *sent.shape[1:])
    )
    sent = sent.reshape(nx * ny * nc, *sent.shape[3:])
    got = lax.all_to_all(sent, ("x", "y", "c"), 0, 0, tiled=True)
    got = lax.all_to_all(
        join_stats(got, nz * nc), ("z", "c"), 0, 0, tiled=True
    )
    got = got.reshape(-1, got.shape[-1])
    mine = lax.dynamic_slice_in_dim(got, at, each, 1)
    return covariance(mine, got[:, LANES:])


def solution(mesh):
    split = Mesh(mesh.devices.reshape(4, 8, 4, 2), ("x", "z", "y", "c"))
    draw, vocab = ("x", "z"), ("y", "c")
    placed = (P(draw, None, None), P(draw, vocab), P())
    return jax.shard_map(
        body, mesh=split, in_specs=placed, out_specs=P(draw, None), check_vma=False
    )
```

```python
import functools

import jax
import jax.numpy as jnp
from jax import lax
from jax.experimental import pallas as pl
from jax.experimental.pallas import tpu as pltpu
from jax.sharding import Mesh
from jax.sharding import PartitionSpec as P

TRAIN = 256
LANES = 128
WIDTHS = (1280, 1152)
WIDTH = sum(WIDTHS)
WIDEST = 1280
CHUNK = 32


def shift(x, axis, by):
    size = lax.axis_size(axis)
    return lax.ppermute(x, axis, [(i, (i + by) % size) for i in range(size)])


def loss_kernel(place_ref, wanted_ref, *refs, sizes, counts):
    pieces = len(sizes)
    inputs = refs[:pieces]
    out_ref, rows_ref, held, weights, logits, top, total, picked, sems = refs[pieces:]
    tokens = wanted_ref.shape[0]
    rows_each = top.shape[0]
    blocks = held.shape[0] // rows_each
    width_all = weights.shape[1]
    tiles = [min(WIDEST, width_all - at) for at in range(0, width_all, WIDEST)]
    starts = [sum(tiles[:k]) for k in range(len(tiles))]

    tile_copies, block_copies = [[]], []
    used = 0
    for k in range(counts[0]):
        lo = 0 if inputs[k].shape[1] == WIDTHS[0] else WIDTHS[0]
        rows = pl.ds(pl.multiple_of(place_ref[k], 16), sizes[k])
        piece = weights.at[rows, lo : lo + inputs[k].shape[1]]
        tile_copies[0].append(pltpu.make_async_copy(inputs[k], piece, sems.at[used]))
        used += 1
    k = counts[0]
    for count in counts[1:]:
        block_copies.append([])
        for _ in range(count):
            rows = pl.ds(pl.multiple_of(place_ref[k], 16), sizes[k])
            block_copies[-1].append(
                pltpu.make_async_copy(inputs[k], held.at[rows, :], sems.at[used])
            )
            used, k = used + 1, k + 1
    order = [*tile_copies, *block_copies]
    for group in order:
        for copy in group:
            copy.start()
    limit = place_ref[pieces]

    def product(slot, block, at, width):
        rows = held[pl.ds(pl.multiple_of(block * rows_each, 16), rows_each), :]
        logits[slot, :, :width] = jnp.dot(
            rows, weights[:, at : at + width], preferred_element_type=jnp.float32
        )

    def absorb(slot, at, width):
        for r in range(0, rows_each, CHUNK):
            some = slice(r, r + CHUNK)
            wanted = wanted_ref[r % tokens : r % tokens + CHUNK, :]
            chosen = picked[some, :] if at else jnp.zeros((CHUNK, LANES), jnp.float32)
            parts = []
            for g in range(0, width, LANES):
                part = logits[slot, some, g : g + LANES]
                chosen = jnp.where(wanted == at + g, part, chosen)
                if at + g >= width_all - 2 * LANES:
                    lane = lax.broadcasted_iota(jnp.int32, part.shape, 1)
                    part = jnp.where(lane + (at + g) < limit, part, -jnp.inf)
                parts.append(part)
            high = parts[0]
            for part in parts[1:]:
                high = jnp.maximum(high, part)
            summed = jnp.zeros((CHUNK, LANES), jnp.float32)
            if at:
                before = top[some, :]
                high = jnp.maximum(high, before)
                summed = total[some, :] * jnp.exp(before - high)
            for part in parts:
                summed = summed + jnp.exp(part - high)
            top[some, :] = high
            total[some, :] = summed
            picked[some, :] = chosen

    def finish(block):
        for r in range(0, rows_each, LANES):
            some = slice(r, r + LANES)
            lane = lax.broadcasted_iota(jnp.int32, (LANES, LANES), 1)
            high = jnp.max(top[some, :], axis=1, keepdims=True)
            summed = total[some, :] * jnp.exp(top[some, :] - high)
            summed = jnp.sum(summed, axis=1, keepdims=True)
            chosen = jnp.sum(picked[some, :], axis=1, keepdims=True)
            both = jnp.transpose(jnp.where(lane == 0, high + jnp.log(summed), chosen))
            high, chosen = both[0:1, :], both[1:2, :]
            row = place_ref[pieces + 1 + block] + r // tokens
            at = slice(r % tokens, r % tokens + LANES)
            rows_ref[row, :, at] = high
            rows_ref[row + 4, :, at] = chosen

    last = (2, starts[-1], tiles[-1])

    def one_block(block, carry):
        def wait(at_block, group):
            @pl.when(block == at_block)
            def _():
                for copy in group:
                    copy.wait()

        for k, group in enumerate(block_copies):
            wait(k, group)
        product(0, block, starts[0], tiles[0])
        absorb(*last)
        finish(jnp.maximum(block - 1, 0))
        for step in range(1, len(tiles)):
            slot = 2 if step == len(tiles) - 1 else step % 2
            product(slot, block, starts[step], tiles[step])
            absorb((step - 1) % 2, starts[step - 1], tiles[step - 1])
        return carry

    for group in tile_copies:
        for copy in group:
            copy.wait()
    lax.fori_loop(0, blocks, one_block, 0)
    absorb(*last)
    finish(blocks - 1)
    receivers, each, _ = out_ref.shape
    for core in range(2):
        rows = [rows_ref[core * each + k] for k in range(each)]
        rows = jnp.concatenate(rows, axis=0)
        for group in range(TRAIN // LANES):
            part = rows[:, group * LANES : (group + 1) * LANES]
            part = jnp.concatenate([part, rows[:, TRAIN:]], axis=1)
            members = receivers * LANES // TRAIN
            for k in range(group * members + core, (group + 1) * members, 2):
                out_ref[k] = part


def cut_columns(matrix, count):
    rows, columns = matrix.shape

    def kernel(in_ref, out_ref):
        for k in range(count):
            size = min(WIDTH, columns - k * WIDTH)
            if size < WIDTH:
                out_ref[k] = jnp.zeros((rows, WIDTH), jnp.bfloat16)
            out_ref[k, :, :size] = in_ref[:, k * WIDTH : k * WIDTH + size]

    vmem = pl.BlockSpec(memory_space=pltpu.VMEM)
    return pl.pallas_call(
        kernel,
        out_shape=jax.ShapeDtypeStruct((count, rows, WIDTH), jnp.bfloat16),
        in_specs=[vmem],
        out_specs=vmem,
    )(matrix)


def join_rows(blocks):
    count, each, width = blocks.shape
    rows, slot = count * each, 32

    def kernel(in_ref, *refs):
        *out_refs, apart = refs
        row = lax.broadcasted_iota(jnp.int32, (rows, count * slot), 0)
        column = lax.broadcasted_iota(jnp.int32, (rows, count * slot), 1)
        chooser = sum(
            (
                (column - k * slot == row - k * each)
                & (column >= k * slot)
                & (column < k * slot + each)
            ).astype(jnp.float32)
            for k in range(count)
        ).astype(jnp.bfloat16)
        apart[...] = jnp.zeros_like(apart)
        for k in range(count):
            apart[k * slot : k * slot + each, :] = in_ref[k]
        at = 0
        for out_ref in out_refs:
            size = out_ref.shape[1]
            out_ref[...] = jnp.dot(
                chooser, apart[:, at : at + size], preferred_element_type=jnp.float32
            ).astype(jnp.bfloat16)
            at += size

    vmem = pl.BlockSpec(memory_space=pltpu.VMEM)
    return pl.pallas_call(
        kernel,
        out_shape=[jax.ShapeDtypeStruct((rows, w), jnp.bfloat16) for w in WIDTHS],
        in_specs=[vmem],
        out_specs=[vmem] * len(WIDTHS),
        scratch_shapes=[pltpu.VMEM((count * slot, width), jnp.bfloat16)],
    )(blocks)


def join_stats(got, copies):
    half = got.shape[1] // 2

    def kernel(in_ref, out_ref):
        parts = in_ref[...]
        high = jnp.max(parts, axis=0)
        logs = high + jnp.log(jnp.sum(jnp.exp(parts - high[None]), axis=0))
        losses = logs[:half] - jnp.sum(parts, axis=0)[half:]
        for k in range(copies):
            out_ref[k] = losses

    vmem = pl.BlockSpec(memory_space=pltpu.VMEM)
    return pl.pallas_call(
        kernel,
        out_shape=jax.ShapeDtypeStruct((copies, half, got.shape[2]), jnp.float32),
        in_specs=[vmem],
        out_specs=vmem,
    )(got)


def local_stats(depth_pieces, row_blocks, place, wanted, receivers):
    width = WIDTH
    depth = row_blocks[0][0].shape[-1]
    rows_each = sum(a.shape[0] for a in row_blocks[0])
    blocks = len(row_blocks)
    tokens = wanted.shape[0]
    rows_total = blocks * rows_each
    groups = [list(depth_pieces), *row_blocks]
    pieces = [piece for group in groups for piece in group]
    sizes = tuple(a.shape[0] for a in pieces)
    counts = tuple(len(group) for group in groups)
    state = pltpu.VMEM((rows_each, LANES), jnp.float32)
    return pl.pallas_call(
        functools.partial(loss_kernel, sizes=sizes, counts=counts),
        out_shape=jax.ShapeDtypeStruct(
            (receivers, rows_total // tokens, tokens - TRAIN + LANES), jnp.float32
        ),
        in_specs=[
            pl.BlockSpec(memory_space=pltpu.SMEM),
            pl.BlockSpec(memory_space=pltpu.VMEM),
        ]
        + [pl.BlockSpec(memory_space=pl.ANY)] * len(pieces),
        out_specs=pl.BlockSpec(memory_space=pltpu.VMEM),
        scratch_shapes=[
            pltpu.VMEM((2 * rows_total // tokens, 1, tokens), jnp.float32),
            pltpu.VMEM((rows_total, depth), jnp.bfloat16),
            pltpu.VMEM((depth, width), jnp.bfloat16),
            pltpu.VMEM((3, rows_each, WIDEST), jnp.float32),
            state,
            state,
            state,
            pltpu.SemaphoreType.DMA((len(pieces),)),
        ],
        compiler_params=pltpu.CompilerParams(vmem_limit_bytes=36 * 2**20),
        cost_estimate=pl.CostEstimate(
            flops=2 * blocks * rows_each * depth * width,
            bytes_accessed=2 * depth * (blocks * rows_each + width),
            transcendentals=blocks * rows_each * width,
        ),
    )(place, wanted, *pieces)


def covariance(train_losses, query_losses):
    train_centered = train_losses - jnp.mean(train_losses, axis=0, keepdims=True)
    query_centered = query_losses - jnp.mean(query_losses, axis=0, keepdims=True)
    draw_count = train_losses.shape[0]
    return jnp.dot(
        train_centered.T,
        query_centered,
        precision=lax.Precision.HIGHEST,
        preferred_element_type=jnp.float32,
    ) / (draw_count - 1.0)


def body(hidden, unembed, targets):
    draws, tokens, model_width = hidden.shape
    depth_each, columns = unembed.shape
    nx, nz = lax.axis_size("x"), lax.axis_size("z")
    ny, nc = lax.axis_size("y"), lax.axis_size("c")
    x, z, y, c = (lax.axis_index(name) for name in ("x", "z", "y", "c"))

    span = nx * depth_each
    blocks = cut_columns(unembed, nx)
    own = lax.all_to_all(blocks, "x", 0, 0, tiled=True)

    source = jnp.arange(model_width, dtype=jnp.int32)
    zp, rest = source // span, source % span
    source = (rest // depth_each * nz + zp) * depth_each + rest % depth_each
    chooser = (
        lax.broadcasted_iota(jnp.int32, (model_width, model_width), 0)
        == source[None, :]
    ).astype(jnp.bfloat16)
    ordered = jnp.dot(
        hidden.reshape(draws * tokens, model_width),
        chooser,
        preferred_element_type=jnp.float32,
    ).astype(jnp.bfloat16)
    mine = lax.dynamic_slice_in_dim(ordered, c * tokens, tokens, 0)

    steps = range(1, nz // 2)
    depth_spots = [z, *((z + s * k) % nz for k in steps for s in (-1, 1)), z + nz // 2]
    depth_spots = [(at + nz) % nz * span for at in depth_spots]
    row_spots = [0]
    for k in range(1, nx):
        row_spots += [(k * draws + c) * tokens, (k * draws + 1 - c) * tokens]
    out_spots = [(x + k) % nx for k in (0, nx - 1, 1, 2)]
    out_spots = [at // nc * (4 * draws) + at % nc * draws for at in out_spots]
    limit = jnp.minimum(columns - x * WIDTH, WIDTH)
    place = jnp.stack(
        [
            jnp.asarray(at, jnp.int32)
            for at in (*depth_spots, *depth_spots, *row_spots, limit, *out_spots)
        ]
    )
    first_column = (y * nc + c) * columns + x * WIDTH
    wanted = (
        targets[:, None]
        - first_column
        - lax.broadcasted_iota(jnp.int32, (tokens, LANES), 1)
    )
    each = TRAIN // (nx * nz)
    mine_at = ((x * nz + z) * each % LANES).astype(jnp.uint32)
    own, place, wanted, mine_at = lax.optimization_barrier(
        (own, place, wanted, mine_at)
    )

    depth_pieces = []
    for half, part in enumerate(join_rows(own)):
        depth_pieces.append(part)
        up = down = part
        for k in steps:
            up = shift(up, "z", 1)
            down = shift(down, "z", -1)
            depth_pieces += [up, down]
        far = (up, 1) if not half else (down, -1)
        depth_pieces.append(shift(far[0], "z", far[1]))
    left, right = shift(mine, "x", 1), shift(mine, "x", -1)
    row_blocks = [[ordered]]
    for rows in (left, right, shift(left, "x", 1)):
        row_blocks.append([rows, shift(rows, "c", 1)])

    sent = local_stats(depth_pieces, row_blocks, place, wanted, nx * ny * nc)
    got = lax.all_to_all(sent, ("x", "y", "c"), 0, 0, tiled=True)
    got = lax.all_to_all(
        join_stats(got, nz * nc), ("z", "c"), 0, 0, tiled=True
    )
    got = got.reshape(-1, got.shape[-1])
    mine = lax.dynamic_slice_in_dim(got, mine_at, each, 1)
    return covariance(mine, got[:, LANES:])


def solution(mesh):
    split = Mesh(mesh.devices.reshape(4, 8, 4, 2), ("x", "z", "y", "c"))
    draw, vocab = ("x", "z"), ("y", "c")
    placed = (P(draw, None, None), P(draw, vocab), P())
    return jax.shard_map(
        body, mesh=split, in_specs=placed, out_specs=P(draw, None), check_vma=False
    )
```

```python
import functools

import jax
import jax.numpy as jnp
from jax import lax
from jax.experimental import pallas as pl
from jax.experimental.pallas import tpu as pltpu
from jax.sharding import Mesh
from jax.sharding import PartitionSpec as P

TRAIN = 256
LANES = 128
WIDTHS = (1280, 1152)
WIDTH = sum(WIDTHS)
WIDEST = 1280
CHUNK = 32


def shift(x, axis, by):
    size = lax.axis_size(axis)
    return lax.ppermute(x, axis, [(i, (i + by) % size) for i in range(size)])


def loss_kernel(place_ref, wanted_ref, *refs, sizes, counts):
    pieces = len(sizes)
    inputs = refs[:pieces]
    out_ref, rows_ref, held, weights, logits, top, total, picked, sems = refs[pieces:]
    tokens = wanted_ref.shape[0]
    rows_each = top.shape[0]
    blocks = held.shape[0] // rows_each
    width_all = weights.shape[1]
    tiles = [min(WIDEST, width_all - at) for at in range(0, width_all, WIDEST)]
    starts = [sum(tiles[:k]) for k in range(len(tiles))]

    tile_copies, block_copies = [[]], []
    used = 0
    for k in range(counts[0]):
        lo = 0 if inputs[k].shape[1] == WIDTHS[0] else WIDTHS[0]
        rows = pl.ds(pl.multiple_of(place_ref[k], 16), sizes[k])
        piece = weights.at[rows, lo : lo + inputs[k].shape[1]]
        tile_copies[0].append(pltpu.make_async_copy(inputs[k], piece, sems.at[used]))
        used += 1
    k = counts[0]
    for count in counts[1:]:
        block_copies.append([])
        for _ in range(count):
            rows = pl.ds(pl.multiple_of(place_ref[k], 16), sizes[k])
            block_copies[-1].append(
                pltpu.make_async_copy(inputs[k], held.at[rows, :], sems.at[used])
            )
            used, k = used + 1, k + 1
    order = [*tile_copies, *block_copies]
    for group in order:
        for copy in group:
            copy.start()
    limit = place_ref[pieces]

    def product(slot, block, at, width):
        rows = held[pl.ds(pl.multiple_of(block * rows_each, 16), rows_each), :]
        logits[slot, :, :width] = jnp.dot(
            rows, weights[:, at : at + width], preferred_element_type=jnp.float32
        )

    def absorb(slot, at, width):
        for r in range(0, rows_each, CHUNK):
            some = slice(r, r + CHUNK)
            wanted = wanted_ref[r % tokens : r % tokens + CHUNK, :]
            chosen = picked[some, :] if at else jnp.zeros((CHUNK, LANES), jnp.float32)
            parts = []
            for g in range(0, width, LANES):
                part = logits[slot, some, g : g + LANES]
                chosen = jnp.where(wanted == at + g, part, chosen)
                if at + g >= width_all - 2 * LANES:
                    lane = lax.broadcasted_iota(jnp.int32, part.shape, 1)
                    part = jnp.where(lane + (at + g) < limit, part, -jnp.inf)
                parts.append(part)
            high = parts[0]
            for part in parts[1:]:
                high = jnp.maximum(high, part)
            summed = jnp.zeros((CHUNK, LANES), jnp.float32)
            if at:
                before = top[some, :]
                high = jnp.maximum(high, before)
                summed = total[some, :] * jnp.exp(before - high)
            for part in parts:
                summed = summed + jnp.exp(part - high)
            top[some, :] = high
            total[some, :] = summed
            picked[some, :] = chosen

    def finish(block):
        for r in range(0, rows_each, LANES):
            some = slice(r, r + LANES)
            lane = lax.broadcasted_iota(jnp.int32, (LANES, LANES), 1)
            high = jnp.max(top[some, :], axis=1, keepdims=True)
            summed = total[some, :] * jnp.exp(top[some, :] - high)
            summed = jnp.sum(summed, axis=1, keepdims=True)
            chosen = jnp.sum(picked[some, :], axis=1, keepdims=True)
            both = jnp.transpose(jnp.where(lane == 0, high + jnp.log(summed), chosen))
            high, chosen = both[0:1, :], both[1:2, :]
            row = place_ref[pieces + 1 + block] + r // tokens
            at = slice(r % tokens, r % tokens + LANES)
            rows_ref[row, :, at] = high
            rows_ref[row + 4, :, at] = chosen

    last = (2, starts[-1], tiles[-1])

    def one_block(block, carry):
        def wait(at_block, group):
            @pl.when(block == at_block)
            def _():
                for copy in group:
                    copy.wait()

        for k, group in enumerate(block_copies):
            wait(k, group)
        product(0, block, starts[0], tiles[0])
        absorb(*last)
        finish(jnp.maximum(block - 1, 0))
        for step in range(1, len(tiles)):
            slot = 2 if step == len(tiles) - 1 else step % 2
            product(slot, block, starts[step], tiles[step])
            absorb((step - 1) % 2, starts[step - 1], tiles[step - 1])
        return carry

    for group in tile_copies:
        for copy in group:
            copy.wait()
    lax.fori_loop(0, blocks, one_block, 0)
    absorb(*last)
    finish(blocks - 1)
    receivers, each, _ = out_ref.shape
    for core in range(2):
        rows = [rows_ref[core * each + k] for k in range(each)]
        rows = jnp.concatenate(rows, axis=0)
        for group in range(TRAIN // LANES):
            part = rows[:, group * LANES : (group + 1) * LANES]
            part = jnp.concatenate([part, rows[:, TRAIN:]], axis=1)
            members = receivers * LANES // TRAIN
            for k in range(group * members + core, (group + 1) * members, 2):
                out_ref[k] = part


def cut_columns(matrix, count, first):
    rows, columns = matrix.shape

    def kernel(first_ref, in_ref, *refs):
        *out_refs, held = refs
        for k in range(count):
            size = min(WIDTH, columns - k * WIDTH)
            if size < WIDTH:
                held[k] = jnp.zeros((rows, WIDTH), jnp.bfloat16)
            held[k, :, :size] = in_ref[:, k * WIDTH : k * WIDTH + size]
        for k, out_ref in enumerate(out_refs):
            out_ref[...] = held[lax.rem(first_ref[0] + k, count)]

    vmem = pl.BlockSpec(memory_space=pltpu.VMEM)
    return pl.pallas_call(
        kernel,
        out_shape=[jax.ShapeDtypeStruct((rows, WIDTH), jnp.bfloat16)] * count,
        in_specs=[pl.BlockSpec(memory_space=pltpu.SMEM), vmem],
        out_specs=[vmem] * count,
        scratch_shapes=[pltpu.VMEM((count, rows, WIDTH), jnp.bfloat16)],
    )(first, matrix)


def join_rows(blocks, first):
    count = len(blocks)
    each, width = blocks[0].shape
    rows, slot = count * each, 32

    def kernel(first_ref, *refs):
        in_refs, out_refs, apart = refs[:count], refs[count:-1], refs[-1]
        row = lax.broadcasted_iota(jnp.int32, (rows, count * slot), 0)
        column = lax.broadcasted_iota(jnp.int32, (rows, count * slot), 1)
        chooser = jnp.zeros((rows, count * slot), jnp.float32)
        for k in range(count):
            place = lax.rem(first_ref[0] - k + count, count) * each
            chooser += (
                (column - k * slot == row - place)
                & (column >= k * slot)
                & (column < k * slot + each)
            ).astype(jnp.float32)
        chooser = chooser.astype(jnp.bfloat16)
        apart[...] = jnp.zeros_like(apart)
        for k in range(count):
            apart[k * slot : k * slot + each, :] = in_refs[k][...]
        at = 0
        for k, size in enumerate(WIDTHS):
            part = jnp.dot(
                chooser, apart[:, at : at + size], preferred_element_type=jnp.float32
            ).astype(jnp.bfloat16)
            out_refs[2 * k][...] = part
            out_refs[2 * k + 1][...] = part
            at += size

    vmem = pl.BlockSpec(memory_space=pltpu.VMEM)
    return pl.pallas_call(
        kernel,
        out_shape=[
            kind((rows, w), jnp.bfloat16)
            for w in WIDTHS
            for kind in (jax.ShapeDtypeStruct, pltpu.VMEM)
        ],
        in_specs=[pl.BlockSpec(memory_space=pltpu.SMEM)] + [vmem] * count,
        out_specs=[vmem] * (2 * len(WIDTHS)),
        scratch_shapes=[pltpu.VMEM((count * slot, width), jnp.bfloat16)],
    )(first, *blocks)


def local_stats(depth_pieces, row_blocks, place, wanted, receivers):
    width = WIDTH
    depth = row_blocks[0][0].shape[-1]
    rows_each = sum(a.shape[0] for a in row_blocks[0])
    blocks = len(row_blocks)
    tokens = wanted.shape[0]
    rows_total = blocks * rows_each
    groups = [list(depth_pieces), *row_blocks]
    pieces = [piece for group in groups for piece in group]
    sizes = tuple(a.shape[0] for a in pieces)
    counts = tuple(len(group) for group in groups)
    state = pltpu.VMEM((rows_each, LANES), jnp.float32)
    return pl.pallas_call(
        functools.partial(loss_kernel, sizes=sizes, counts=counts),
        out_shape=jax.ShapeDtypeStruct(
            (receivers, rows_total // tokens, tokens - TRAIN + LANES), jnp.float32
        ),
        in_specs=[
            pl.BlockSpec(memory_space=pltpu.SMEM),
            pl.BlockSpec(memory_space=pltpu.VMEM),
        ]
        + [pl.BlockSpec(memory_space=pl.ANY)] * len(pieces),
        out_specs=pl.BlockSpec(memory_space=pltpu.VMEM),
        scratch_shapes=[
            pltpu.VMEM((2 * rows_total // tokens, 1, tokens), jnp.float32),
            pltpu.VMEM((rows_total, depth), jnp.bfloat16),
            pltpu.VMEM((depth, width), jnp.bfloat16),
            pltpu.VMEM((3, rows_each, WIDEST), jnp.float32),
            state,
            state,
            state,
            pltpu.SemaphoreType.DMA((len(pieces),)),
        ],
        compiler_params=pltpu.CompilerParams(vmem_limit_bytes=36 * 2**20),
        cost_estimate=pl.CostEstimate(
            flops=2 * blocks * rows_each * depth * width,
            bytes_accessed=2 * depth * (blocks * rows_each + width),
            transcendentals=blocks * rows_each * width,
        ),
    )(place, wanted, *pieces)


def covariance(train_losses, query_losses):
    train_centered = train_losses - jnp.mean(train_losses, axis=0, keepdims=True)
    query_centered = query_losses - jnp.mean(query_losses, axis=0, keepdims=True)
    draw_count = train_losses.shape[0]
    return jnp.dot(
        train_centered.T,
        query_centered,
        precision=lax.Precision.HIGHEST,
        preferred_element_type=jnp.float32,
    ) / (draw_count - 1.0)


def body(hidden, unembed, targets):
    draws, tokens, model_width = hidden.shape
    depth_each, columns = unembed.shape
    nx, nz = lax.axis_size("x"), lax.axis_size("z")
    ny, nc = lax.axis_size("y"), lax.axis_size("c")
    x, z, y, c = (lax.axis_index(name) for name in ("x", "z", "y", "c"))

    span = nx * depth_each
    own = [
        shift(block, "x", k) if k else block
        for k, block in enumerate(cut_columns(unembed, nx, x.reshape(1)))
    ]

    source = jnp.arange(model_width, dtype=jnp.int32)
    zp, rest = source // span, source % span
    source = (rest // depth_each * nz + zp) * depth_each + rest % depth_each
    chooser = (
        lax.broadcasted_iota(jnp.int32, (model_width, model_width), 0)
        == source[None, :]
    ).astype(jnp.bfloat16)
    ordered = jnp.dot(
        hidden.reshape(draws * tokens, model_width),
        chooser,
        preferred_element_type=jnp.float32,
    ).astype(jnp.bfloat16)
    mine = lax.dynamic_slice_in_dim(ordered, c * tokens, tokens, 0)

    steps = range(1, nz // 2)
    depth_spots = [z, *((z + s * k) % nz for k in steps for s in (-1, 1)), z + nz // 2]
    depth_spots = [(at + nz) % nz * span for at in depth_spots]
    row_spots = [0]
    for k in range(1, nx):
        row_spots += [(k * draws + c) * tokens, (k * draws + 1 - c) * tokens]
    out_spots = [(x + k) % nx for k in (0, nx - 1, 1, 2)]
    out_spots = [at // nc * (4 * draws) + at % nc * draws for at in out_spots]
    limit = jnp.minimum(columns - x * WIDTH, WIDTH)
    place = jnp.stack(
        [
            jnp.asarray(at, jnp.int32)
            for at in (*depth_spots, *depth_spots, *row_spots, limit, *out_spots)
        ]
    )
    first_column = (y * nc + c) * columns + x * WIDTH
    wanted = (
        targets[:, None]
        - first_column
        - lax.broadcasted_iota(jnp.int32, (tokens, LANES), 1)
    )
    each = TRAIN // (nx * nz)
    mine_at = ((x * nz + z) * each % LANES).astype(jnp.uint32)
    own, place, wanted, mine_at = lax.optimization_barrier(
        (own, place, wanted, mine_at)
    )

    depth_pieces = []
    joined = join_rows(own, x.reshape(1))
    for half, (part, kept) in enumerate((joined[:2], joined[2:])):
        depth_pieces.append(kept)
        up = down = part
        for k in steps:
            up = shift(up, "z", 1)
            down = shift(down, "z", -1)
            depth_pieces += [up, down]
        far = (up, 1) if not half else (down, -1)
        depth_pieces.append(shift(far[0], "z", far[1]))
    left, right = shift(mine, "x", 1), shift(mine, "x", -1)
    row_blocks = [[ordered]]
    for rows in (left, right, shift(left, "x", 1)):
        row_blocks.append([rows, shift(rows, "c", 1)])

    sent = local_stats(depth_pieces, row_blocks, place, wanted, nx * ny * nc)
    got = lax.all_to_all(sent, ("x", "y", "c"), 0, 0, tiled=True)
    logs, chosen = got[:, : 2 * draws], got[:, 2 * draws :]
    high = jnp.max(logs, axis=0)
    losses = (
        high
        + jnp.log(jnp.sum(jnp.exp(logs - high[None]), axis=0))
        - jnp.sum(chosen, axis=0)
    )
    got = lax.all_to_all(
        jnp.broadcast_to(losses[None], (nz * nc, *losses.shape)),
        ("z", "c"),
        0,
        0,
        tiled=True,
    )
    got = got.reshape(-1, got.shape[-1])
    mine = lax.dynamic_slice_in_dim(got, mine_at, each, 1)
    return covariance(mine, got[:, LANES:])


def solution(mesh):
    split = Mesh(mesh.devices.reshape(4, 8, 4, 2), ("x", "z", "y", "c"))
    draw, vocab = ("x", "z"), ("y", "c")
    placed = (P(draw, None, None), P(draw, vocab), P())
    return jax.shard_map(
        body, mesh=split, in_specs=placed, out_specs=P(draw, None), check_vma=False
    )
```

```python
import functools

import jax
import jax.numpy as jnp
from jax import lax
from jax.experimental import pallas as pl
from jax.experimental.pallas import tpu as pltpu
from jax.sharding import Mesh
from jax.sharding import PartitionSpec as P

TRAIN = 256
LANES = 128
WIDTHS = (1280, 1152)
WIDTH = sum(WIDTHS)
EARLY = 512
WIDEST = 1280
CHUNK = 32


def shift(x, axis, by):
    size = lax.axis_size(axis)
    return lax.ppermute(x, axis, [(i, (i + by) % size) for i in range(size)])


def loss_kernel(place_ref, wanted_ref, begun_ref, *refs, sizes, counts):
    pieces = len(sizes)
    inputs = refs[:pieces]
    out_ref, rows_ref, held, weights, logits, top, total, picked, sems = refs[pieces:]
    tokens = wanted_ref.shape[0]
    rows_each = top.shape[0]
    blocks = held.shape[0] // rows_each
    width_all = weights.shape[1]
    tiles = [min(WIDEST, width_all - at) for at in range(0, width_all, WIDEST)]
    starts = [sum(tiles[:k]) for k in range(len(tiles))]

    tile_copies, block_copies = [[]], []
    used = 0
    for k in range(counts[0]):
        lo = 0 if inputs[k].shape[1] == WIDTHS[0] else WIDTHS[0]
        rows = pl.ds(pl.multiple_of(place_ref[k], 16), sizes[k])
        piece = weights.at[rows, lo : lo + inputs[k].shape[1]]
        tile_copies[0].append(pltpu.make_async_copy(inputs[k], piece, sems.at[used]))
        used += 1
    k = counts[0]
    for count in counts[1:]:
        block_copies.append([])
        for _ in range(count):
            rows = pl.ds(pl.multiple_of(place_ref[k], 16), sizes[k])
            block_copies[-1].append(
                pltpu.make_async_copy(inputs[k], held.at[rows, :], sems.at[used])
            )
            used, k = used + 1, k + 1
    order = [*tile_copies, *block_copies]
    for group in order:
        for copy in group:
            copy.start()
    limit = place_ref[pieces]

    def product(slot, block, at, width, first):
        rows = held[pl.ds(pl.multiple_of(block * rows_each, 16), rows_each), :]
        done = EARLY if first else 0
        tile = jnp.dot(
            rows[:, done:],
            weights[done:, at : at + width],
            preferred_element_type=jnp.float32,
        )
        logits[slot, :, :width] = (
            tile + begun_ref[:, at : at + width] if first else tile
        )

    def absorb(slot, at, width):
        for r in range(0, rows_each, CHUNK):
            some = slice(r, r + CHUNK)
            wanted = wanted_ref[r % tokens : r % tokens + CHUNK, :]
            chosen = picked[some, :] if at else jnp.zeros((CHUNK, LANES), jnp.float32)
            parts = []
            for g in range(0, width, LANES):
                part = logits[slot, some, g : g + LANES]
                chosen = jnp.where(wanted == at + g, part, chosen)
                if at + g >= width_all - 2 * LANES:
                    lane = lax.broadcasted_iota(jnp.int32, part.shape, 1)
                    part = jnp.where(lane + (at + g) < limit, part, -jnp.inf)
                parts.append(part)
            high = parts[0]
            for part in parts[1:]:
                high = jnp.maximum(high, part)
            summed = jnp.zeros((CHUNK, LANES), jnp.float32)
            if at:
                before = top[some, :]
                high = jnp.maximum(high, before)
                summed = total[some, :] * jnp.exp(before - high)
            for part in parts:
                summed = summed + jnp.exp(part - high)
            top[some, :] = high
            total[some, :] = summed
            picked[some, :] = chosen

    def finish(block):
        for r in range(0, rows_each, LANES):
            some = slice(r, r + LANES)
            lane = lax.broadcasted_iota(jnp.int32, (LANES, LANES), 1)
            high = jnp.max(top[some, :], axis=1, keepdims=True)
            summed = total[some, :] * jnp.exp(top[some, :] - high)
            summed = jnp.sum(summed, axis=1, keepdims=True)
            chosen = jnp.sum(picked[some, :], axis=1, keepdims=True)
            both = jnp.transpose(jnp.where(lane == 0, high + jnp.log(summed), chosen))
            high, chosen = both[0:1, :], both[1:2, :]
            row = place_ref[pieces + 1 + block] + r // tokens
            at = slice(r % tokens, r % tokens + LANES)
            rows_ref[row, :, at] = high
            rows_ref[row + 4, :, at] = chosen

    last = (2, starts[-1], tiles[-1])

    def one_block(block, carry, first=False):
        if first:
            for copy in block_copies[0]:
                copy.wait()
        for k, group in enumerate(block_copies[1:]):
            if not first:

                @pl.when(block == k + 1)
                def _():
                    for copy in group:
                        copy.wait()

        product(0, block, starts[0], tiles[0], first)
        if not first:
            absorb(*last)
            finish(block - 1)
        for step in range(1, len(tiles)):
            slot = 2 if step == len(tiles) - 1 else step % 2
            product(slot, block, starts[step], tiles[step], first)
            absorb((step - 1) % 2, starts[step - 1], tiles[step - 1])
        return carry

    for group in tile_copies:
        for copy in group:
            copy.wait()
    one_block(0, 0, first=True)
    lax.fori_loop(1, blocks, one_block, 0)
    absorb(*last)
    finish(blocks - 1)
    receivers, each, _ = out_ref.shape
    for core in range(2):
        rows = [rows_ref[core * each + k] for k in range(each)]
        rows = jnp.concatenate(rows, axis=0)
        for group in range(TRAIN // LANES):
            part = rows[:, group * LANES : (group + 1) * LANES]
            part = jnp.concatenate([part, rows[:, TRAIN:]], axis=1)
            members = receivers * LANES // TRAIN
            for k in range(group * members + core, (group + 1) * members, 2):
                out_ref[k] = part


def cut_columns(matrix, count, first):
    rows, columns = matrix.shape

    def kernel(first_ref, in_ref, *refs):
        *out_refs, held = refs
        for k in range(count):
            size = min(WIDTH, columns - k * WIDTH)
            if size < WIDTH:
                held[k] = jnp.zeros((rows, WIDTH), jnp.bfloat16)
            held[k, :, :size] = in_ref[:, k * WIDTH : k * WIDTH + size]
        for k, out_ref in enumerate(out_refs):
            out_ref[...] = held[lax.rem(first_ref[0] + k, count)]

    vmem = pl.BlockSpec(memory_space=pltpu.VMEM)
    return pl.pallas_call(
        kernel,
        out_shape=[jax.ShapeDtypeStruct((rows, WIDTH), jnp.bfloat16)] * count,
        in_specs=[pl.BlockSpec(memory_space=pltpu.SMEM), vmem],
        out_specs=[vmem] * count,
        scratch_shapes=[pltpu.VMEM((count, rows, WIDTH), jnp.bfloat16)],
    )(first, matrix)


def join_rows(blocks, first):
    count = len(blocks)
    each, width = blocks[0].shape
    rows, slot = count * each, 32

    def kernel(first_ref, *refs):
        in_refs, out_refs, apart = refs[:count], refs[count:-1], refs[-1]
        row = lax.broadcasted_iota(jnp.int32, (rows, count * slot), 0)
        column = lax.broadcasted_iota(jnp.int32, (rows, count * slot), 1)
        chooser = jnp.zeros((rows, count * slot), jnp.float32)
        for k in range(count):
            place = lax.rem(first_ref[0] - k + count, count) * each
            chooser += (
                (column - k * slot == row - place)
                & (column >= k * slot)
                & (column < k * slot + each)
            ).astype(jnp.float32)
        chooser = chooser.astype(jnp.bfloat16)
        apart[...] = jnp.zeros_like(apart)
        for k in range(count):
            apart[k * slot : k * slot + each, :] = in_refs[k][...]
        at = 0
        for k, size in enumerate(WIDTHS):
            part = jnp.dot(
                chooser, apart[:, at : at + size], preferred_element_type=jnp.float32
            ).astype(jnp.bfloat16)
            out_refs[2 * k][...] = part
            out_refs[2 * k + 1][...] = part
            at += size

    vmem = pl.BlockSpec(memory_space=pltpu.VMEM)
    return pl.pallas_call(
        kernel,
        out_shape=[
            kind((rows, w), jnp.bfloat16)
            for w in WIDTHS
            for kind in (jax.ShapeDtypeStruct, pltpu.VMEM)
        ],
        in_specs=[pl.BlockSpec(memory_space=pltpu.SMEM)] + [vmem] * count,
        out_specs=[vmem] * (2 * len(WIDTHS)),
        scratch_shapes=[pltpu.VMEM((count * slot, width), jnp.bfloat16)],
    )(first, *blocks)


def begin_products(rows, *halves):
    count, depth = rows.shape[0], sum(piece.shape[0] for piece in halves[0])
    pieces = [piece for half in halves for piece in half]

    def kernel(rows_ref, *refs):
        inputs, (out_ref, held, weights, sems) = refs[: len(pieces)], refs[len(pieces) :]
        copies = [pltpu.make_async_copy(rows_ref, held, sems.at[len(pieces)])]
        for k, piece in enumerate(inputs):
            size, width = piece.shape
            half, place = divmod(k, len(pieces) // len(halves))
            columns = slice(half * WIDTHS[0], half * WIDTHS[0] + width)
            spot = weights.at[place * size : (place + 1) * size, columns]
            copies.append(pltpu.make_async_copy(piece, spot, sems.at[k]))
        for copy in copies:
            copy.start()
        for copy in copies:
            copy.wait()
        for at in range(0, WIDTH, 512):
            to = min(at + 512, WIDTH)
            out_ref[:, at:to] = jnp.dot(
                held[:, :EARLY], weights[:EARLY, at:to], preferred_element_type=jnp.float32
            )

    return pl.pallas_call(
        kernel,
        out_shape=pltpu.VMEM((count, WIDTH), jnp.float32),
        in_specs=[pl.BlockSpec(memory_space=pl.ANY)] * (1 + len(pieces)),
        out_specs=pl.BlockSpec(memory_space=pltpu.VMEM),
        scratch_shapes=[
            pltpu.VMEM(rows.shape, jnp.bfloat16),
            pltpu.VMEM((depth, WIDTH), jnp.bfloat16),
            pltpu.SemaphoreType.DMA((1 + len(pieces),)),
        ],
        compiler_params=pltpu.CompilerParams(vmem_limit_bytes=16 * 2**20),
        cost_estimate=pl.CostEstimate(
            flops=2 * count * EARLY * WIDTH,
            bytes_accessed=2 * rows.size + 2 * depth * WIDTH,
            transcendentals=0,
        ),
    )(rows, *pieces)


def local_stats(depth_pieces, row_blocks, place, wanted, begun, receivers):
    width = WIDTH
    depth = row_blocks[0][0].shape[-1]
    rows_each = sum(a.shape[0] for a in row_blocks[0])
    blocks = len(row_blocks)
    tokens = wanted.shape[0]
    rows_total = blocks * rows_each
    groups = [list(depth_pieces), *row_blocks]
    pieces = [piece for group in groups for piece in group]
    sizes = tuple(a.shape[0] for a in pieces)
    counts = tuple(len(group) for group in groups)
    state = pltpu.VMEM((rows_each, LANES), jnp.float32)
    return pl.pallas_call(
        functools.partial(loss_kernel, sizes=sizes, counts=counts),
        out_shape=jax.ShapeDtypeStruct(
            (receivers, rows_total // tokens, tokens - TRAIN + LANES), jnp.float32
        ),
        in_specs=[
            pl.BlockSpec(memory_space=pltpu.SMEM),
            pl.BlockSpec(memory_space=pltpu.VMEM),
            pl.BlockSpec(memory_space=pltpu.VMEM),
        ]
        + [pl.BlockSpec(memory_space=pl.ANY)] * len(pieces),
        out_specs=pl.BlockSpec(memory_space=pltpu.VMEM),
        scratch_shapes=[
            pltpu.VMEM((2 * rows_total // tokens, 1, tokens), jnp.float32),
            pltpu.VMEM((rows_total, depth), jnp.bfloat16),
            pltpu.VMEM((depth, width), jnp.bfloat16),
            pltpu.VMEM((3, rows_each, WIDEST), jnp.float32),
            state,
            state,
            state,
            pltpu.SemaphoreType.DMA((len(pieces),)),
        ],
        compiler_params=pltpu.CompilerParams(vmem_limit_bytes=36 * 2**20),
        cost_estimate=pl.CostEstimate(
            flops=2 * blocks * rows_each * depth * width,
            bytes_accessed=2 * depth * (blocks * rows_each + width),
            transcendentals=blocks * rows_each * width,
        ),
    )(place, wanted, begun, *pieces)


def covariance(train_losses, query_losses):
    train_centered = train_losses - jnp.mean(train_losses, axis=0, keepdims=True)
    query_centered = query_losses - jnp.mean(query_losses, axis=0, keepdims=True)
    draw_count = train_losses.shape[0]
    return jnp.dot(
        train_centered.T,
        query_centered,
        precision=lax.Precision.HIGHEST,
        preferred_element_type=jnp.float32,
    ) / (draw_count - 1.0)


def body(hidden, unembed, targets):
    draws, tokens, model_width = hidden.shape
    depth_each, columns = unembed.shape
    nx, nz = lax.axis_size("x"), lax.axis_size("z")
    ny, nc = lax.axis_size("y"), lax.axis_size("c")
    x, z, y, c = (lax.axis_index(name) for name in ("x", "z", "y", "c"))

    span = nx * depth_each
    own = [
        shift(block, "x", k) if k else block
        for k, block in enumerate(cut_columns(unembed, nx, x.reshape(1)))
    ]

    source = jnp.arange(model_width, dtype=jnp.int32)
    turn, rest = source // span, source % span
    zp = (z + jnp.where(turn % 2 == 1, nz - (turn + 1) // 2, turn // 2)) % nz
    source = (rest // depth_each * nz + zp) * depth_each + rest % depth_each
    chooser = (
        lax.broadcasted_iota(jnp.int32, (model_width, model_width), 0)
        == source[None, :]
    ).astype(jnp.bfloat16)
    ordered = jnp.dot(
        hidden.reshape(draws * tokens, model_width),
        chooser,
        preferred_element_type=jnp.float32,
    ).astype(jnp.bfloat16)
    mine = lax.dynamic_slice_in_dim(ordered, c * tokens, tokens, 0)

    steps = range(1, nz // 2)
    depth_spots = [k * span for k in range(nz)]
    row_spots = [0]
    for k in range(1, nx):
        row_spots += [(k * draws + c) * tokens, (k * draws + 1 - c) * tokens]
    out_spots = [(x + k) % nx for k in (0, nx - 1, 1, 2)]
    out_spots = [at // nc * (4 * draws) + at % nc * draws for at in out_spots]
    limit = jnp.minimum(columns - x * WIDTH, WIDTH)
    place = jnp.stack(
        [
            jnp.asarray(at, jnp.int32)
            for at in (*depth_spots, *depth_spots, *row_spots, limit, *out_spots)
        ]
    )
    first_column = (y * nc + c) * columns + x * WIDTH
    wanted = (
        targets[:, None]
        - first_column
        - lax.broadcasted_iota(jnp.int32, (tokens, LANES), 1)
    )
    each = TRAIN // (nx * nz)
    mine_at = ((x * nz + z) * each % LANES).astype(jnp.uint32)
    own, place, wanted, mine_at = lax.optimization_barrier(
        (own, place, wanted, mine_at)
    )

    depth_pieces = []
    joined = join_rows(own, x.reshape(1))
    for half, (part, kept) in enumerate((joined[:2], joined[2:])):
        depth_pieces.append(kept)
        up = down = part
        for k in steps:
            up = shift(up, "z", 1)
            down = shift(down, "z", -1)
            depth_pieces += [up, down]
        far = (up, 1) if not half else (down, -1)
        depth_pieces.append(shift(far[0], "z", far[1]))
    begun = begin_products(ordered, depth_pieces[:5], depth_pieces[nz : nz + 5])
    left, right = shift(mine, "x", 1), shift(mine, "x", -1)
    row_blocks = [[ordered]]
    for rows in (left, right, shift(left, "x", 1)):
        row_blocks.append([rows, shift(rows, "c", 1)])

    sent = local_stats(
        depth_pieces, row_blocks, place, wanted, begun, nx * ny * nc
    )
    got = lax.all_to_all(sent, ("x", "y", "c"), 0, 0, tiled=True)
    logs, chosen = got[:, : 2 * draws], got[:, 2 * draws :]
    high = jnp.max(logs, axis=0)
    losses = (
        high
        + jnp.log(jnp.sum(jnp.exp(logs - high[None]), axis=0))
        - jnp.sum(chosen, axis=0)
    )
    got = lax.all_to_all(
        jnp.broadcast_to(losses[None], (nz * nc, *losses.shape)),
        ("z", "c"),
        0,
        0,
        tiled=True,
    )
    got = got.reshape(-1, got.shape[-1])
    mine = lax.dynamic_slice_in_dim(got, mine_at, each, 1)
    return covariance(mine, got[:, LANES:])


def solution(mesh):
    split = Mesh(mesh.devices.reshape(4, 8, 4, 2), ("x", "z", "y", "c"))
    draw, vocab = ("x", "z"), ("y", "c")
    placed = (P(draw, None, None), P(draw, vocab), P())
    return jax.shard_map(
        body, mesh=split, in_specs=placed, out_specs=P(draw, None), check_vma=False
    )
```
